32 devices in a mesh: seq: 4 (over y, x), fsdp: 8 (over z, core).
Axes of the slice: x: 2, y: 2, z: 4, core: 2. Of those that a mesh axis runs over, the one named last changes fastest.
Arguments:
- stream: float32 [8, 512, 1024], P('fsdp', 'seq'), may hold values from -6 to 6
- cotangent: float32 [8, 512, 1024], P('fsdp', 'seq'), may hold values from -6 to 6
- prenorm: bfloat16 [1024], P('fsdp'), may hold values from 0.5 to 1.5
- mixing: bfloat16 [1024, 6144], P('fsdp'), may hold values from -0.1875 to 0.1875
- ratemap: bfloat16 [1024, 16], P('fsdp'), may hold values from -0.1875 to 0.1875
- convtaps: bfloat16 [4, 4096], P(None, 'fsdp'), may hold values from -3 to 3
- decaylog: float32 [8], replicated, may hold values from -6 to 1
- decaybias: float32 [8], replicated, may hold values from -3 to 1
- headgain: bfloat16 [256], P('fsdp'), may hold values from 0.5 to 1.5
- outmap: bfloat16 [2048, 1024], P('fsdp'), may hold values from -0.1875 to 0.1875
- postnorm: bfloat16 [1024], P('fsdp'), may hold values from 0.5 to 1.5
- upmap: bfloat16 [1024, 5632], P('fsdp'), may hold values from -0.1875 to 0.1875
- downmap: bfloat16 [2816, 1024], P('fsdp'), may hold values from -0.15625 to 0.15625
Outputs:
- result: float32 [8, 512, 1024], P('fsdp', 'seq')
- stream_grad: float32 [8, 512, 1024], P('fsdp', 'seq')
- prenorm_grad: float32 [1024], P('fsdp')
- mixing_grad: float32 [1024, 6144], P('fsdp')
- ratemap_grad: float32 [1024, 16], P('fsdp')
- convtaps_grad: float32 [4, 4096], P(None, 'fsdp')
- decaylog_grad: float32 [8], replicated
- decaybias_grad: float32 [8], replicated
- headgain_grad: float32 [256], P('fsdp')
- outmap_grad: float32 [2048, 1024], P('fsdp')
- postnorm_grad: float32 [1024], P('fsdp')
- upmap_grad: float32 [1024, 5632], P('fsdp')
- downmap_grad: float32 [2816, 1024], P('fsdp')
The draws below stay inside these ranges and needn't reach their ends.
All inputs are finite; a program needn't handle non-finite values.
Results may differ from the reference program's by a relative error of at most 0.025.
Values may be sent and summed in bfloat16 or wider, within the bound.
No kernel may reach another device: no remote copies, remote signals or barrier semaphores. Data moves between devices by JAX's collectives and lax.ppermute only.
A program may use at most 256 MiB of HBM per device.

```python
import jax
import jax.numpy as jnp
from jax import lax

D = 1024
H = 8
DK = 128
DV = 256
FF = 2816
CONV = 4
SPAN = 64
SEQ_LEN = 512
SEQS = 8
QKV = 4096
VW = 2048
MIX = 6144


def level_of(stream_key, dims, cuts, least, top_value):
    level = 1.0
    for axis_at, blocks in cuts:
        steps = jax.random.uniform(jax.random.fold_in(jax.random.fold_in(stream_key, 6), axis_at), (blocks,), jnp.float32, least / len(cuts), top_value / len(cuts))
        level = level * jnp.repeat(jnp.exp(steps), dims[axis_at] // blocks).reshape((-1,) + (1,) * (len(dims) - 1 - axis_at))
    return level


def gaussian(rng, dims, width, reach, split=(), held_as=jnp.bfloat16):
    factor_of = level_of(rng, dims, split, -0.22, 0.18) if split else 1.0
    drawn = jax.random.normal(rng, dims, jnp.float32) * width * factor_of
    return jnp.minimum(jnp.maximum(drawn, -reach), reach).astype(held_as)


def setup_inputs(seed: int = 0) -> dict:
    seeds = jax.random.split(jax.random.key(seed), 14)
    stream = gaussian(seeds[0], (SEQS, SEQ_LEN, D), 1.0, 6.0, ((0, 8), (1, 4)), jnp.float32)
    cotangent = gaussian(seeds[1], (SEQS, SEQ_LEN, D), 1.0, 6.0, ((0, 8), (1, 4)), jnp.float32)
    prenorm = jnp.clip(1.0 + 0.1 * jax.random.normal(seeds[2], (D,), jnp.float32), 0.5, 1.5).astype(jnp.bfloat16)
    mixing = gaussian(seeds[3], (D, MIX), D ** -0.5, 0.1875, ((0, 8),))
    ratemap = gaussian(seeds[4], (D, 2 * H), D ** -0.5, 0.1875, ((0, 8),))
    convtaps = gaussian(seeds[5], (CONV, QKV), CONV ** -0.5, 3.0, ((1, 8),))
    decaylog = jnp.clip(jax.random.uniform(seeds[6], (H,), jnp.float32, -6.0, 1.0), -6.0, 1.0)
    decaybias = jnp.clip(jax.random.uniform(seeds[7], (H,), jnp.float32, -3.0, 1.0), -3.0, 1.0)
    headgain = jnp.clip(1.0 + 0.1 * jax.random.normal(seeds[8], (DV,), jnp.float32), 0.5, 1.5).astype(jnp.bfloat16)
    outmap = gaussian(seeds[9], (VW, D), (VW // 2) ** -0.5, 0.1875, ((0, 8),))
    postnorm = jnp.clip(1.0 + 0.1 * jax.random.normal(seeds[10], (D,), jnp.float32), 0.5, 1.5).astype(jnp.bfloat16)
    upmap = gaussian(seeds[11], (D, 2 * FF), D ** -0.5, 0.1875, ((0, 8),))
    downmap = gaussian(seeds[12], (FF, D), (FF // 2) ** -0.5, 0.15625, ((0, 8),))
    return {"stream": stream, "cotangent": cotangent, "prenorm": prenorm, "mixing": mixing, "ratemap": ratemap, "convtaps": convtaps, "decaylog": decaylog, "decaybias": decaybias, "headgain": headgain, "outmap": outmap, "postnorm": postnorm, "upmap": upmap, "downmap": downmap}


HIGHEST = lax.Precision.HIGHEST
EPSILON = 1e-06

def norm_rows(values, gain):
    return values * lax.rsqrt(lax.optimization_barrier(jnp.mean(values * values, axis=-1, keepdims=True)) + EPSILON) * gain

def product(left, right):
    return jnp.dot(left.astype(jnp.float32), right.astype(jnp.float32), preferred_element_type=jnp.float32)

def outer_sum(left, right):
    return lax.dot_general(left.astype(jnp.float32), right.astype(jnp.float32), (((0,), (0,)), ((), ())), preferred_element_type=jnp.float32)

def back_product(left, right):
    return lax.dot_general(left.astype(jnp.float32), right.astype(jnp.float32), (((1,), (1,)), ((), ())), preferred_element_type=jnp.float32)

def prepare(extended, conv_taps, rate_logits, decay_log, decay_bias):
    length = extended.shape[0] - (CONV - 1)
    filtered = conv_taps[0] * extended[0:length]
    for offset in range(1, CONV):
        filtered = filtered + conv_taps[offset] * extended[offset:offset + length]
    activated = filtered * jax.nn.sigmoid(filtered)
    queries = activated[:, :H * DK].reshape(length, H, DK)
    keys_raw = activated[:, H * DK:2 * H * DK].reshape(length, H, DK)
    values = activated[:, 2 * H * DK:].reshape(length, H, DV)
    queries = queries * lax.rsqrt(lax.optimization_barrier(jnp.sum(queries * queries, axis=-1, keepdims=True)) + EPSILON) * DK ** (-0.5)
    keys_unit = keys_raw * lax.rsqrt(lax.optimization_barrier(jnp.sum(keys_raw * keys_raw, axis=-1, keepdims=True)) + EPSILON)
    strength = jax.nn.sigmoid(rate_logits[:, :H])
    decays = -jnp.exp(decay_log) * jax.nn.softplus(rate_logits[:, H:] + decay_bias)
    return (queries, keys_unit, values, strength, decays)

def span_terms(queries, keys_unit, values, strength, decays):
    size_block = queries.shape[0]
    cumulative = jnp.cumsum(decays, axis=0)
    log_gap = cumulative[:, None, :] - cumulative[None, :, :]
    row_index = jnp.arange(size_block)[:, None, None]
    col_index = jnp.arange(size_block)[None, :, None]
    below = row_index > col_index
    causal = row_index >= col_index
    fade_below = jnp.where(below, jnp.exp(jnp.where(below, log_gap, 0.0)), 0.0)
    fade_causal = jnp.where(causal, jnp.exp(jnp.where(causal, log_gap, 0.0)), 0.0)
    key_key = jnp.einsum('thd,shd->tsh', keys_unit, keys_unit, precision=HIGHEST)
    query_key = jnp.einsum('thd,shd->tsh', queries, keys_unit, precision=HIGHEST)
    system = jnp.transpose(strength[:, None, :] * fade_below * key_key, (2, 0, 1)) + jnp.eye(size_block, dtype=queries.dtype)
    scaled = jnp.exp(cumulative)
    right_keys = jnp.transpose((strength * scaled)[:, :, None] * keys_unit, (1, 0, 2))
    right_values = jnp.transpose(strength[:, :, None] * values, (1, 0, 2))
    weight_keys = lax.linalg.triangular_solve(system, right_keys, left_side=True, lower=True, unit_diagonal=True)
    weight_values = lax.linalg.triangular_solve(system, right_values, left_side=True, lower=True, unit_diagonal=True)
    end_fade = jnp.exp(cumulative[-1][None, :] - cumulative)
    return (weight_keys, weight_values, scaled[:, :, None] * queries, fade_causal * query_key, end_fade[:, :, None] * keys_unit, jnp.exp(cumulative[-1]))

def span_out(piece, carried):
    weight_keys, weight_values, queries_scaled, attend, keys_scaled, end_gain = piece
    fresh = weight_values - jnp.einsum('hck,hvk->hcv', weight_keys, carried, precision=HIGHEST)
    output = jnp.einsum('chk,hvk->chv', queries_scaled, carried, precision=HIGHEST)
    output = output + jnp.einsum('tsh,hsv->thv', attend, fresh, precision=HIGHEST)
    following = end_gain[:, None, None] * carried + jnp.einsum('hcv,chk->hvk', fresh, keys_scaled, precision=HIGHEST)
    return (output, following)

def advance_block(carried, piece):
    output, following = span_out(piece, carried)
    return (following, output)

def to_blocks(arrays):
    return tuple((member.reshape((member.shape[0] // SPAN, SPAN) + member.shape[1:]) for member in arrays))

def run_core(queries, keys_unit, values, strength, decays, start_state):
    length = queries.shape[0]
    pieces = jax.vmap(span_terms)(*to_blocks((queries, keys_unit, values, strength, decays)))
    final_state, outs_blocks = lax.scan(advance_block, start_state, pieces)
    return (outs_blocks.reshape(length, H, DV), final_state)

def gate_norm(heads_out, gate_in, head_gain):
    length = heads_out.shape[0]
    normed = heads_out * lax.rsqrt(lax.optimization_barrier(jnp.mean(heads_out * heads_out, axis=-1, keepdims=True)) + EPSILON) * head_gain
    gate_heads = gate_in.reshape(length, H, DV)
    return (normed * gate_heads * jax.nn.sigmoid(gate_heads)).reshape(length, H * DV)

def reference(stream, cotangent, prenorm, mixing, ratemap, convtaps, decaylog, decaybias, headgain, outmap, postnorm, upmap, downmap):
    pre_gain = prenorm.astype(jnp.float32)
    conv_taps = convtaps.astype(jnp.float32)
    head_gain = headgain.astype(jnp.float32)
    post_gain = postnorm.astype(jnp.float32)
    qkv_width = convtaps.shape[1]

    def one_sequence(totals, pair):
        inputs, out_cot = pair
        normed = norm_rows(inputs, pre_gain).astype(jnp.bfloat16)
        projected = product(normed, mixing)
        pre_conv = projected[:, :qkv_width].astype(jnp.bfloat16)
        gate_in = projected[:, qkv_width:]
        rate_logits = product(normed, ratemap)
        extended = jnp.concatenate([jnp.zeros((CONV - 1, qkv_width), jnp.float32), pre_conv.astype(jnp.float32)], axis=0)
        prepared = prepare(extended, conv_taps, rate_logits, decaylog, decaybias)
        empty_state = jnp.zeros((H, DV, DK), jnp.float32)
        heads_out, _ = run_core(*prepared, empty_state)
        gated = gate_norm(heads_out, gate_in, head_gain).astype(jnp.bfloat16)
        hidden = inputs + product(gated, outmap)
        post_normed = norm_rows(hidden, post_gain).astype(jnp.bfloat16)
        both_parts = product(post_normed, upmap)
        gate_part = both_parts[:, :FF]
        up_part = both_parts[:, FF:]
        sigmoid_gate = jax.nn.sigmoid(gate_part)
        mlp_act = (gate_part * sigmoid_gate * up_part).astype(jnp.bfloat16)
        output = hidden + product(mlp_act, downmap)
        cot_bf = out_cot.astype(jnp.bfloat16)
        grad_down = outer_sum(mlp_act, cot_bf)
        back_act = back_product(cot_bf, downmap)
        back_gate_part = back_act * up_part * sigmoid_gate * (1.0 + gate_part * (1.0 - sigmoid_gate))
        back_up_part = back_act * gate_part * sigmoid_gate
        back_both = jnp.concatenate([back_gate_part, back_up_part], axis=1).astype(jnp.bfloat16)
        grad_up = outer_sum(post_normed, back_both)
        back_post = back_product(back_both, upmap)
        _, pull_post = jax.vjp(norm_rows, hidden, post_gain)
        back_hidden_norm, grad_post = pull_post(back_post)
        back_hidden = out_cot + back_hidden_norm
        hidden_bf = back_hidden.astype(jnp.bfloat16)
        grad_out = outer_sum(gated, hidden_bf)
        back_gated = back_product(hidden_bf, outmap)
        _, pull_gate = jax.vjp(gate_norm, heads_out, gate_in, head_gain)
        back_heads, back_gate, grad_head = pull_gate(back_gated)
        _, pull_core = jax.vjp(run_core, *prepared, empty_state)
        core_grads = pull_core((back_heads, empty_state))
        _, pull_prep = jax.vjp(prepare, extended, conv_taps, rate_logits, decaylog, decaybias)
        back_ext, grad_conv, back_rates, grad_dlog, grad_dbias = pull_prep(core_grads[:5])
        back_proj = jnp.concatenate([back_ext[CONV - 1:], back_gate], axis=1).astype(jnp.bfloat16)
        rates_bf = back_rates.astype(jnp.bfloat16)
        grad_mix = outer_sum(normed, back_proj)
        grad_rate = outer_sum(normed, rates_bf)
        back_normed = back_product(back_proj, mixing) + back_product(rates_bf, ratemap)
        _, pull_pre = jax.vjp(norm_rows, inputs, pre_gain)
        back_inputs, grad_pre = pull_pre(back_normed)
        input_grad = back_hidden + back_inputs
        grads = (grad_pre, grad_mix, grad_rate, grad_conv, grad_dlog, grad_dbias, grad_head, grad_out, grad_post, grad_up, grad_down)
        return (jax.tree.map(jnp.add, totals, grads), (output, input_grad))
    shapes = [(D,), (D, MIX), (D, 2 * H), (CONV, QKV), (H,), (H,), (DV,), (VW, D), (D,), (D, 2 * FF), (FF, D)]
    zeros = tuple((jnp.zeros(shape_one, jnp.float32) for shape_one in shapes))
    totals, (outputs, input_grads) = lax.scan(one_sequence, zeros, (stream, cotangent))
    return (outputs, input_grads, totals[0], totals[1], totals[2], totals[3], totals[4], totals[5], totals[6], totals[7], totals[8], totals[9], totals[10])
```

```python
import functools

import jax
import jax.numpy as jnp
from jax import lax
from jax.experimental import pallas as pl
from jax.experimental.pallas import tpu as pltpu
from jax.sharding import PartitionSpec as P

CHUNK = 128
LANES = 128
PAD = 8
EPSILON = 1e-06
F32 = jnp.float32
BF16 = jnp.bfloat16
INTERPRET = False
UNROLL = 1
PASSES = {"inv": 3, "kk": 3, "qk": 3, "chain": 3, "out": 3, "back": 3, "grad": 3}


def halves(value):
    high = value.astype(BF16)
    return high, (value - high.astype(F32)).astype(BF16)


def contract(left, right, dims, site):
    def dot(a, b):
        return lax.dot_general(a, b, (dims, ((), ())), preferred_element_type=F32)

    if PASSES[site] == 1:
        return dot(left.astype(BF16), right.astype(BF16))
    left, right = halves(left), halves(right)
    return dot(left[0], right[0]) + (dot(left[0], right[1]) + dot(left[1], right[0]))


def mm(left, right, site):
    return contract(left, right, ((1,), (0,)), site)


def mt(left, right, site):
    return contract(left, right, ((1,), (1,)), site)


def tm(left, right, site):
    return contract(left, right, ((0,), (0,)), site)


def thirds(value):
    high, rest = halves(value)
    low = (value - high.astype(F32) - rest.astype(F32)).astype(BF16)
    return high, rest, low


def exact(flags, value, dims, flags_first=True):
    total = None
    for part in thirds(value)[::-1]:
        pair = (flags, part) if flags_first else (part, flags)
        term = lax.dot_general(*pair, (dims, ((), ())), preferred_element_type=F32)
        total = term if total is None else total + term
    return total


def sigmoid(value):
    return 1.0 / (1.0 + jnp.exp(-value))


def soft_plus(value):
    return jnp.maximum(value, 0.0) + jnp.log1p(jnp.exp(-jnp.abs(value)))


def rates_of(logits, decay_ref, heads):
    lane = lax.broadcasted_iota(jnp.int32, logits.shape, 1)
    decays = decay_ref[0:1] * soft_plus(logits + decay_ref[1:2])
    return jnp.where(lane < heads, sigmoid(logits), decays)


def iotas(size):
    rows = lax.broadcasted_iota(jnp.int32, (size, size), 0)
    cols = lax.broadcasted_iota(jnp.int32, (size, size), 1)
    return rows, cols


def unit_inverse(lower, rows, cols):
    size = lower.shape[0]
    inverse = jnp.where(rows == cols, 1.0, 0.0) - jnp.where(rows // 2 == cols // 2, lower, 0.0)
    width = 2
    while width < size:
        joins = (rows // (2 * width) == cols // (2 * width)) & (rows // width != cols // width)
        inverse = inverse - mm(mm(inverse, jnp.where(joins, lower, 0.0), "inv"), inverse, "inv")
        width *= 2
    return inverse


def conv_window(window, taps, span):
    total = taps[0:1] * window[PAD - 3 : PAD - 3 + span]
    for offset in range(1, 4):
        start = PAD - 3 + offset
        total = total + taps[offset : offset + 1] * window[start : start + span]
    return total


def fades(decay, rows, cols):
    span = rows.shape[0]
    ones_below = jnp.where(rows >= cols, 1.0, 0.0).astype(BF16)
    wide = jnp.broadcast_to(decay, (span, span))
    by_row = exact(ones_below, wide, ((1,), (0,)))
    by_col = exact(ones_below, wide, ((0,), (1,)), False)
    gap = by_row - by_col
    causal = rows >= cols
    fade = jnp.where(causal, jnp.exp(jnp.where(causal, gap, 0.0)), 0.0)
    total = by_row[span - 1 : span, 0:1]
    grown = jnp.exp(by_row[:, 0:1])
    left = jnp.exp(total - by_row[:, 0:1])
    return fade, grown, left, jnp.exp(total)


def forward_kernel(
    pre_ref, gate_ref, logit_ref, decay_ref, taps_ref, gain_ref,
    gated_ref, out_ref, fresh_ref, state_ref, inv_ref, att_ref,
    xp, qs, kb, ke, vb, rate_ref, carried, *, heads, dk, dv, chunk
):
    length = pre_ref.shape[0]
    size = chunk
    blocks = length // size
    qw = heads * dk
    xp[0:PAD] = jnp.zeros((PAD, xp.shape[1]), F32)
    xp[PAD:] = pre_ref[...].astype(F32)
    carried[...] = jnp.zeros_like(carried)
    rate_ref[...] = rates_of(logit_ref[...], decay_ref, heads)
    rows, cols = iotas(size)

    def prepare(i, carry):
        r0 = pl.multiple_of(i * size, size)
        rates = rate_ref[pl.ds(r0, size), :]
        for h in range(heads):
            def act(start, width):
                c = conv_window(xp[pl.ds(r0, size + PAD), start : start + width], taps_ref[:, start : start + width], size)
                return c * sigmoid(c)

            q = act(h * dk, dk)
            k = act(qw + h * dk, dk)
            v = act(2 * qw + h * dv, dv)
            q = q * (lax.rsqrt(jnp.sum(q * q, axis=1, keepdims=True) + EPSILON) * dk ** (-0.5))
            k = k * lax.rsqrt(jnp.sum(k * k, axis=1, keepdims=True) + EPSILON)
            beta = rates[:, h : h + 1]
            fade, grown, left, _ = fades(rates[:, heads + h : heads + h + 1], rows, cols)
            lower = jnp.where(rows > cols, beta * fade * mt(k, k, "kk"), 0.0)
            inv_ref[i, h] = unit_inverse(lower, rows, cols)
            att_ref[i, h] = fade * mt(q, k, "qk")
            span = pl.ds(r0, size)
            qs[span, h * dk : (h + 1) * dk] = grown * q
            kb[span, h * dk : (h + 1) * dk] = (beta * grown) * k
            ke[span, h * dk : (h + 1) * dk] = left * k
            vb[span, h * dv : (h + 1) * dv] = beta * v
        return carry

    lax.fori_loop(0, blocks, prepare, 0, unroll=UNROLL)

    def advance(i, carry):
        r0 = pl.multiple_of(i * size, size)
        span = pl.ds(r0, size)
        rates = rate_ref[span, :]
        for h in range(heads):
            state = carried[h]
            state_ref[i, h] = state
            ks = slice(h * dk, (h + 1) * dk)
            vs = slice(h * dv, (h + 1) * dv)
            fresh = mm(inv_ref[i, h], vb[span, vs] - mm(kb[span, ks], state, "chain"), "chain")
            fresh_ref[span, vs] = fresh
            out = mm(qs[span, ks], state, "out") + mm(att_ref[i, h], fresh, "out")
            out_ref[span, vs] = out
            end = jnp.exp(jnp.sum(rates[:, heads + h : heads + h + 1], axis=0, keepdims=True))
            carried[h] = end * state + tm(ke[span, ks], fresh, "chain")
            scale = lax.rsqrt(jnp.mean(out * out, axis=1, keepdims=True) + EPSILON)
            gate = gate_ref[span, vs]
            gated_ref[span, vs] = (out * scale * gain_ref[...] * gate * sigmoid(gate)).astype(BF16)
        return carry

    lax.fori_loop(0, blocks, advance, 0, unroll=UNROLL)


def backward_kernel(
    pre_ref, gate_ref, logit_ref, decay_ref, taps_ref, gain_ref, out_ref, fresh_ref, state_ref, inv_ref, att_ref, dgated_ref,
    dproj_ref, small_ref,
    xp, qn, kn, vn, dout, dright, dstate, dconv, rate_ref, drate_ref, carried, *, heads, dk, dv, chunk
):
    length = pre_ref.shape[0]
    size = chunk
    blocks = length // size
    qw = heads * dk
    wide = xp.shape[1]
    xp[0:PAD] = jnp.zeros((PAD, wide), F32)
    xp[PAD:] = pre_ref[...].astype(F32)
    dconv[length:] = jnp.zeros((PAD, wide), F32)
    carried[...] = jnp.zeros_like(carried)
    small_ref[...] = jnp.zeros_like(small_ref)
    drate_ref[...] = jnp.zeros_like(drate_ref)
    rate_ref[...] = rates_of(logit_ref[...], decay_ref, heads)
    rows, cols = iotas(size)

    def conv_of(r0, start, width):
        return conv_window(xp[pl.ds(r0, size + PAD), start : start + width], taps_ref[:, start : start + width], size)

    def prepare(i, carry):
        r0 = pl.multiple_of(i * size, size)
        span = pl.ds(r0, size)
        for h in range(heads):
            vs = slice(h * dv, (h + 1) * dv)
            ks = slice(h * dk, (h + 1) * dk)
            c = conv_of(r0, h * dk, dk)
            q = c * sigmoid(c)
            qn[span, ks] = q * (lax.rsqrt(jnp.sum(q * q, axis=1, keepdims=True) + EPSILON) * dk ** (-0.5))
            c = conv_of(r0, qw + h * dk, dk)
            k = c * sigmoid(c)
            kn[span, ks] = k * lax.rsqrt(jnp.sum(k * k, axis=1, keepdims=True) + EPSILON)
            c = conv_of(r0, 2 * qw + h * dv, dv)
            vn[span, vs] = c * sigmoid(c)
            out = out_ref[span, vs]
            scale = lax.rsqrt(jnp.mean(out * out, axis=1, keepdims=True) + EPSILON)
            unit = out * scale
            gate = gate_ref[span, vs]
            sig = sigmoid(gate)
            dz = dgated_ref[span, vs] * gate * sig
            small_ref[4:5, 0:dv] += jnp.sum(dz * unit, axis=0, keepdims=True)
            dn = dz * gain_ref[...]
            dout[span, vs] = scale * (dn - unit * jnp.mean(unit * dn, axis=1, keepdims=True))
        return carry

    lax.fori_loop(0, blocks, prepare, 0, unroll=UNROLL)

    def retreat(step, carry):
        i = blocks - 1 - step
        r0 = pl.multiple_of(i * size, size)
        span = pl.ds(r0, size)
        rates = rate_ref[span, :]
        for h in range(heads):
            vs = slice(h * dv, (h + 1) * dv)
            ks = slice(h * dk, (h + 1) * dk)
            q, k = qn[span, ks], kn[span, ks]
            beta = rates[:, h : h + 1]
            fade, grown, left, end = fades(rates[:, heads + h : heads + h + 1], rows, cols)
            attend = att_ref[i, h]
            after = carried[h]
            dstate[i, h] = after
            do = dout[span, vs]
            dfresh = tm(attend, do, "back") + mm(left * k, after, "back")
            dr = tm(inv_ref[i, h], dfresh, "back")
            dright[span, vs] = dr
            carried[h] = tm(grown * q, do, "back") + end * after - tm((beta * grown) * k, dr, "back")
        return carry

    lax.fori_loop(0, blocks, retreat, 0, unroll=UNROLL)

    def collect(i, carry):
        r0 = pl.multiple_of(i * size, size)
        span = pl.ds(r0, size)
        rates = rate_ref[span, :]
        ones = jnp.ones((size, size), BF16)
        ones_below = jnp.where(rows >= cols, 1.0, 0.0).astype(BF16)
        for h in range(heads):
            vs = slice(h * dv, (h + 1) * dv)
            ks = slice(h * dk, (h + 1) * dk)
            q, k, v = qn[span, ks], kn[span, ks], vn[span, vs]
            beta = rates[:, h : h + 1]
            fade, grown, left, end = fades(rates[:, heads + h : heads + h + 1], rows, cols)
            below = jnp.where(rows > cols, fade, 0.0)
            state, after = state_ref[i, h], dstate[i, h]
            do, dr, fresh = dout[span, vs], dright[span, vs], fresh_ref[span, vs]
            d_att = mt(do, fresh, "grad")
            d_low = -mt(dr, fresh, "grad")
            pairs = below * mt(k, k, "kk")
            scores = att_ref[i, h]
            d_qk = fade * d_att
            d_kk = beta * below * d_low
            d_qs = mt(do, state, "grad")
            d_ke = mt(fresh, after, "grad")
            d_kb = -mt(dr, state, "grad")
            gaps = d_low * (beta * pairs) + d_att * scores
            dbeta = jnp.sum(d_low * pairs, axis=1, keepdims=True)
            dbeta = dbeta + grown * jnp.sum(d_kb * k, axis=1, keepdims=True)
            dbeta = dbeta + jnp.sum(dr * v, axis=1, keepdims=True)
            dq = mm(d_qk, k, "grad") + grown * d_qs
            dk_ = mm(d_kk, k, "grad") + tm(d_kk, k, "grad") + tm(d_qk, q, "grad") + (beta * grown) * d_kb + left * d_ke
            dv_ = beta * dr
            from_end = left * jnp.sum(d_ke * k, axis=1, keepdims=True)
            dcum = jnp.sum(gaps, axis=1, keepdims=True) - exact(ones, gaps, ((0,), (0,)), False)[:, 0:1]
            dcum = dcum + grown * jnp.sum(d_qs * q, axis=1, keepdims=True)
            dcum = dcum + (beta * grown) * jnp.sum(d_kb * k, axis=1, keepdims=True) - from_end
            d_end = jnp.sum(from_end, axis=0, keepdims=True) + end * jnp.sum(
                jnp.sum(state * after, axis=1, keepdims=True), axis=0, keepdims=True
            )
            ddecay = exact(ones_below, jnp.broadcast_to(dcum, (size, size)), ((0,), (0,)))[:, 0:1] + d_end
            drate_ref[span, h : h + 1] = dbeta
            drate_ref[span, heads + h : heads + h + 1] = ddecay

            def back(start, width, grad, factor):
                c = conv_of(r0, start, width)
                sig = sigmoid(c)
                if factor is not None:
                    act = c * sig
                    scale = lax.rsqrt(jnp.sum(act * act, axis=1, keepdims=True) + EPSILON)
                    unit = act * scale
                    grad = grad * factor
                    grad = scale * (grad - unit * jnp.sum(unit * grad, axis=1, keepdims=True))
                dconv[span, start : start + width] = grad * sig * (1.0 + c * (1.0 - sig))

            back(h * dk, dk, dq, dk ** (-0.5))
            back(qw + h * dk, dk, dk_, 1.0)
            back(2 * qw + h * dv, dv, dv_, None)
        return carry

    lax.fori_loop(0, blocks, collect, 0, unroll=UNROLL)

    def unconv(i, carry):
        r0 = pl.multiple_of(i * size, size)
        span = pl.ds(r0, size)
        step = min(256, wide)
        for start in range(0, wide, step):
            cs = slice(start, start + step)
            dwin = dconv[pl.ds(r0, size + PAD), cs]
            xwin = xp[pl.ds(r0, size + PAD), cs]
            taps = taps_ref[:, cs]
            total = None
            for j in range(4):
                term = taps[j : j + 1] * dwin[3 - j : 3 - j + size]
                total = term if total is None else total + term
                small_ref[j : j + 1, cs] += jnp.sum(
                    dwin[0:size] * xwin[PAD - 3 + j : PAD - 3 + j + size], axis=0, keepdims=True
                )
            dproj_ref[span, cs] = total.astype(BF16)
        return carry

    lax.fori_loop(0, blocks, unconv, 0, unroll=UNROLL)
    grads, rates, logits = drate_ref[...], rate_ref[...], logit_ref[...]
    lane = lax.broadcasted_iota(jnp.int32, grads.shape, 1)
    slope = jnp.where(lane < heads, rates * (1.0 - rates), decay_ref[0:1] * sigmoid(logits + decay_ref[1:2]))
    back = grads * slope
    dproj_ref[:, wide:] = back.astype(BF16)
    small_ref[5:6, 0:LANES] = jnp.sum(grads * rates, axis=0, keepdims=True)
    small_ref[6:7, 0:LANES] = jnp.sum(back, axis=0, keepdims=True)


def chunk_of(length):
    chunk = CHUNK
    while length % chunk:
        chunk //= 2
    return chunk


def whole(*dims):
    return pl.BlockSpec((None,) + dims, lambda b: (b,) + (0,) * len(dims))


def fixed(*dims):
    return pl.BlockSpec(dims, lambda b: (0,) * len(dims))


def mix_forward(pre, gate, logits, decay, taps, gain, heads, dk, dv):
    count, length, wide = pre.shape
    chunk = chunk_of(length)
    blocks = length // chunk
    vw = heads * dv
    square = (blocks, heads, chunk, chunk)
    return pl.pallas_call(
        functools.partial(forward_kernel, heads=heads, dk=dk, dv=dv, chunk=chunk),
        grid=(count,),
        in_specs=[
            whole(length, wide), whole(length, vw), whole(length, LANES),
            fixed(*decay.shape), fixed(*taps.shape), fixed(*gain.shape),
        ],
        out_specs=[
            whole(length, vw), whole(length, vw), whole(length, vw), whole(blocks, heads, dk, dv), whole(*square), whole(*square),
        ],
        out_shape=[
            jax.ShapeDtypeStruct((count, length, vw), BF16),
            jax.ShapeDtypeStruct((count, length, vw), F32),
            jax.ShapeDtypeStruct((count, length, vw), F32),
            jax.ShapeDtypeStruct((count, blocks, heads, dk, dv), F32),
            jax.ShapeDtypeStruct((count,) + square, F32),
            jax.ShapeDtypeStruct((count,) + square, F32),
        ],
        scratch_shapes=[
            pltpu.VMEM((length + PAD, wide), F32),
            pltpu.VMEM((length, heads * dk), F32),
            pltpu.VMEM((length, heads * dk), F32),
            pltpu.VMEM((length, heads * dk), F32),
            pltpu.VMEM((length, vw), F32),
            pltpu.VMEM((length, LANES), F32),
            pltpu.VMEM((heads, dk, dv), F32),
        ],
        cost_estimate=pl.CostEstimate(flops=10**10, bytes_accessed=32 * 2**20, transcendentals=10**6),
        interpret=INTERPRET,
    )(pre, gate, logits, decay, taps, gain)


def mix_backward(pre, gate, logits, decay, taps, gain, saved, dgated, heads, dk, dv):
    count, length, wide = pre.shape
    chunk = chunk_of(length)
    blocks = length // chunk
    vw = heads * dv
    square = (blocks, heads, chunk, chunk)
    return pl.pallas_call(
        functools.partial(backward_kernel, heads=heads, dk=dk, dv=dv, chunk=chunk),
        grid=(count,),
        in_specs=[
            whole(length, wide), whole(length, vw), whole(length, LANES),
            fixed(*decay.shape), fixed(*taps.shape), fixed(*gain.shape),
            whole(length, vw), whole(length, vw), whole(blocks, heads, dk, dv), whole(*square), whole(*square), whole(length, vw),
        ],
        out_specs=[whole(length, wide + LANES), whole(8, wide)],
        out_shape=[
            jax.ShapeDtypeStruct((count, length, wide + LANES), BF16),
            jax.ShapeDtypeStruct((count, 8, wide), F32),
        ],
        scratch_shapes=[
            pltpu.VMEM((length + PAD, wide), F32),
            pltpu.VMEM((length, heads * dk), F32),
            pltpu.VMEM((length, heads * dk), F32),
            pltpu.VMEM((length, vw), F32),
            pltpu.VMEM((length, vw), F32),
            pltpu.VMEM((length, vw), F32),
            pltpu.VMEM((blocks, heads, dk, dv), F32),
            pltpu.VMEM((length + PAD, wide), F32),
            pltpu.VMEM((length, LANES), F32),
            pltpu.VMEM((length, LANES), F32),
            pltpu.VMEM((heads, dk, dv), F32),
        ],
        cost_estimate=pl.CostEstimate(flops=10**10, bytes_accessed=32 * 2**20, transcendentals=2 * 10**6),
        interpret=INTERPRET,
    )(pre, gate, logits, decay, taps, gain, *saved, dgated)


def unit_rows(values):
    return values * lax.rsqrt(jnp.mean(values * values, axis=-1, keepdims=True) + EPSILON)


def unit_back(values, grad):
    scale = lax.rsqrt(jnp.mean(values * values, axis=-1, keepdims=True) + EPSILON)
    unit = values * scale
    return scale * (grad - unit * jnp.mean(unit * grad, axis=-1, keepdims=True))


def product(left, right):
    return jnp.dot(left, right, preferred_element_type=F32)


def outer_sum(left, right):
    return lax.dot_general(left, right, (((0,), (0,)), ((), ())), preferred_element_type=F32)


def back_product(left, right):
    return lax.dot_general(left, right, (((1,), (1,)), ((), ())), preferred_element_type=F32)


def cut(array, start, size, axis):
    return lax.dynamic_slice_in_dim(array, start, size, axis)


def after(value, *others):
    return lax.optimization_barrier((value,) + others)[0]


def turned(value, by):
    peers = lax.axis_size("seq")
    return lax.ppermute(value, "seq", [(i, (i + by) % peers) for i in range(peers)])


def sent_round(piece):
    return [turned(piece, by) for by in range(1, lax.axis_size("seq"))]


def place_kernel(order_ref, *refs):
    for turn, piece_ref in enumerate(refs[:-1]):

        @pl.when(pl.program_id(0) == turn)
        def _():
            refs[-1][...] = piece_ref[...]


def in_order(piece, others, axis):
    peers = lax.axis_size("seq")
    flat = (piece.size // piece.shape[-1], piece.shape[-1])
    order = (lax.axis_index("seq") - jnp.arange(peers, dtype=jnp.int32)) % peers
    joined = pl.pallas_call(
        place_kernel,
        grid_spec=pltpu.PrefetchScalarGridSpec(
            num_scalar_prefetch=1,
            grid=(peers,),
            in_specs=[pl.BlockSpec(flat, lambda p, order: (0, 0)) for _ in range(peers)],
            out_specs=pl.BlockSpec((None,) + flat, lambda p, order: (order[p], 0, 0)),
        ),
        out_shape=jax.ShapeDtypeStruct((peers,) + flat, piece.dtype),
        cost_estimate=pl.CostEstimate(flops=0, bytes_accessed=4 * peers * piece.size, transcendentals=0),
        interpret=INTERPRET,
    )(order, *[part.reshape(flat) for part in [piece] + others])
    joined = jnp.moveaxis(joined.reshape((peers,) + piece.shape), 0, axis)
    return joined.reshape(piece.shape[:axis] + (-1,) + piece.shape[axis + 1 :])


def seq_gather(piece, axis=1):
    return in_order(piece, sent_round(piece), axis)


def seq_blocks(partial):
    peers = lax.axis_size("seq")
    here = lax.axis_index("seq")
    length = partial.shape[1] // peers
    others = [turned(cut(partial, ((here + by) % peers) * length, length, 1), by) for by in range(1, peers)]
    return [cut(partial, here * length, length, 1)] + others


def add_up(blocks):
    total = blocks[0].astype(F32)
    for block in blocks[1:]:
        total = total + block.astype(F32)
    return total


def swap_pairs(invert):
    peers, owners = lax.axis_size("seq"), lax.axis_size("fsdp")
    group = owners // peers
    pairs = []
    for s in range(peers):
        for f in range(owners):
            holder = (f % peers) * owners + s * group + f // peers
            pairs.append((s * owners + f, holder) if invert else (holder, s * owners + f))
    return pairs


def owners_piece(shard):
    rows = shard.shape[0] // lax.axis_size("seq")
    return cut(shard, lax.axis_index("seq") * rows, rows, 0)


def small_sum(value):
    owners = lax.axis_size("fsdp")
    step = 1
    while step < owners:
        value = value + lax.ppermute(value, "fsdp", [(i, i ^ step) for i in range(owners)])
        step *= 2
    return value


def pair_parts(grad, rider=None):
    owners = lax.axis_size("fsdp")
    parity = lax.axis_index("fsdp") % 2
    wide = grad.shape[1]
    grad = grad.reshape(owners // 2, 2, -1, wide)
    given = cut(grad, 1 - parity, 1, 1).reshape(-1, wide)
    kept = cut(grad, parity, 1, 1).reshape(-1, wide)
    if rider is None:
        return given, kept
    return jnp.concatenate([given, rider]), jnp.concatenate([kept, rider])


def pair_sent(given):
    return lax.ppermute(given, "fsdp", [(i, i ^ 1) for i in range(lax.axis_size("fsdp"))])


def pair_total(given, kept, riding=0):
    total = (kept.astype(F32) + given.astype(F32)).astype(BF16)
    size = total.shape[0] - riding
    blocks = total[:size].reshape(lax.axis_size("fsdp") // 2, -1, total.shape[1])
    return (blocks, total[size:]) if riding else (blocks,)


def chip_blocks(both, rider=None):
    owners = lax.axis_size("fsdp")
    groups = owners // 2
    place = lax.axis_index("fsdp") // 2

    def block(at):
        part = cut(both, at, 1, 0)[0]
        return part if rider is None else jnp.concatenate([part, rider])

    blocks = [block(place)]
    for by in range(1, groups):
        pairs = [(i, (i + 2 * by) % owners) for i in range(owners)]
        blocks.append(lax.ppermute(block((place + by) % groups), "fsdp", pairs))
    return blocks


def columns(stacked, start, width):
    part = stacked[:, :, start : start + width]
    return jnp.transpose(part, (1, 0, 2)).reshape(part.shape[1], -1)


def shards(
    stream, cotangent, prenorm, mixing, ratemap, convtaps, decaylog, decaybias, headgain, outmap, postnorm, upmap, downmap,
):
    count, length, width = stream.shape
    peers, owners = lax.axis_size("seq"), lax.axis_size("fsdp")
    here = lax.axis_index("seq")
    direct = owners <= 8
    all_heads = decaylog.shape[0]
    heads = all_heads // peers
    dv = headgain.shape[0] * owners
    qkv = convtaps.shape[1] * owners
    dk = (qkv // all_heads - dv) // 2
    kw, vw = heads * dk, heads * dv
    wide = 2 * kw + vw
    core = wide + LANES
    ff = downmap.shape[0] * owners // peers
    tokens = count * length * peers
    by_seq = (count, peers * length)
    held = mixing.shape[0]
    out_held = outmap.shape[0] // peers

    taps_part = convtaps.reshape(held, -1)
    gain_part = jnp.pad(headgain, (0, held - headgain.shape[0]))[:, None]
    used = 2 * heads + taps_part.shape[1] + 1
    mix_part = jnp.concatenate(
        [
            cut(mixing, here * kw, kw, 1),
            cut(mixing, all_heads * dk + here * kw, kw, 1),
            cut(mixing, 2 * all_heads * dk + here * vw, vw, 1),
            cut(ratemap, here * heads, heads, 1),
            cut(ratemap, all_heads + here * heads, heads, 1),
            taps_part,
            gain_part,
            jnp.zeros((held, LANES - used), BF16),
            cut(mixing, qkv + here * vw, vw, 1),
        ],
        axis=1,
    )
    mix = lax.all_gather(mix_part, "fsdp", axis=0, tiled=True)
    gains = after(jnp.stack([prenorm, postnorm]), mix_part)
    gains = lax.all_gather(gains, "fsdp", axis=1, tiled=True).astype(F32)
    pre_gain, post_gain = gains[0], gains[1]

    normed_own = (unit_rows(stream) * pre_gain).astype(BF16)
    both = seq_gather(jnp.concatenate([normed_own, cotangent.astype(BF16)], axis=2))
    rows_piece = jnp.concatenate([owners_piece(outmap), owners_piece(downmap)], axis=0)
    rows_piece = lax.ppermute(rows_piece, ("seq", "fsdp"), swap_pairs(False))
    up_part = jnp.concatenate([cut(upmap, here * ff, ff, 1), cut(upmap, (peers + here) * ff, ff, 1)], axis=1)
    rows_piece, up_part, both, mix = lax.optimization_barrier((rows_piece, up_part, both, mix))
    rows_all = lax.all_gather(rows_piece, "fsdp", axis=0, tiled=False)
    up = lax.all_gather(up_part, "fsdp", axis=0, tiled=True)
    normed = both[:, :, :width].reshape(tokens, width)
    cot_bf = both[:, :, width:].reshape(tokens, width)

    extra = mix[:, wide:core]
    taps_all = extra[:, 2 * heads : 2 * heads + taps_part.shape[1]].reshape(owners, convtaps.shape[0], -1)
    taps_all = jnp.transpose(taps_all, (1, 0, 2)).reshape(convtaps.shape[0], -1)
    taps = jnp.concatenate(
        [
            cut(taps_all, here * kw, kw, 1),
            cut(taps_all, all_heads * dk + here * kw, kw, 1),
            cut(taps_all, 2 * all_heads * dk + here * vw, vw, 1),
        ],
        axis=1,
    ).astype(F32)
    head_gain = extra[:, used - 1].reshape(owners, held)[:, : headgain.shape[0]].reshape(1, dv).astype(F32)
    decay = jnp.stack([-jnp.exp(cut(decaylog, here * heads, heads, 0)), cut(decaybias, here * heads, heads, 0)])
    decay = jnp.pad(decay, ((0, 6), (heads, LANES - 2 * heads)))

    pre = product(normed, mix[:, :wide]).astype(BF16).reshape(by_seq + (wide,))
    gate = product(normed, mix[:, core:]).reshape(by_seq + (vw,))
    logits = product(normed, extra).reshape(by_seq + (LANES,))
    gated, *saved = mix_forward(pre, gate, logits, decay, taps, head_gain, heads, dk, dv)
    gated = gated.reshape(tokens, vw)
    out_rows = rows_all[:, :out_held].reshape(vw, width)
    down = rows_all[:, out_held:].reshape(ff, width)
    hidden = stream + add_up(seq_blocks(product(gated, out_rows).astype(BF16).reshape(by_seq + (width,))))

    post_own = (unit_rows(hidden) * post_gain).astype(BF16)
    post_sent = sent_round(post_own)
    back_act = back_product(cot_bf, down)
    *post_sent, back_act = lax.optimization_barrier((*post_sent, back_act))
    post = in_order(post_own, post_sent, 1).reshape(tokens, width)
    gate_part = product(post, up[:, :ff])
    up_half = product(post, up[:, ff:])
    sig = jax.nn.sigmoid(gate_part)
    mlp_act = (gate_part * sig * up_half).astype(BF16)
    back_gate = (back_act * up_half * sig * (1.0 + gate_part * (1.0 - sig))).astype(BF16)
    back_up = (back_act * gate_part * sig).astype(BF16)
    back_both = jnp.concatenate([back_gate, back_up], axis=1)
    back_part, back_both = lax.optimization_barrier((back_product(back_both, up).astype(BF16), back_both))
    back_blocks = seq_blocks(back_part.reshape(by_seq + (width,)))
    grad_up = outer_sum(post, back_both).astype(BF16)
    *back_blocks, token = lax.optimization_barrier((*back_blocks, grad_up))
    grad_up = lax.psum_scatter(grad_up, "fsdp", scatter_dimension=0, tiled=True)
    back_hidden = cotangent + unit_back(hidden, add_up(back_blocks) * post_gain)
    hidden_own = back_hidden.astype(BF16)
    hidden_sent = sent_round(hidden_own)
    mlp_act_late = after(mlp_act, token)
    grad_down = outer_sum(mlp_act_late, cot_bf).astype(BF16)
    mlp_out = product(mlp_act_late, down).astype(BF16).reshape(by_seq + (width,))
    *hidden_sent, mlp_out, grad_down = lax.optimization_barrier((*hidden_sent, mlp_out, grad_down))
    hidden_bf = in_order(hidden_own, hidden_sent, 1).reshape(tokens, width)
    grad_down = lax.psum_scatter(grad_down, "fsdp", scatter_dimension=0, tiled=True)

    back_gated = back_product(hidden_bf, out_rows).reshape(by_seq + (vw,))
    out_units = unit_rows(saved[0].reshape(by_seq + (heads, dv))) * head_gain
    gate_heads = gate.reshape(by_seq + (heads, dv))
    gate_sig = jax.nn.sigmoid(gate_heads)
    back_gate_in = back_gated.reshape(gate_heads.shape) * out_units * gate_sig * (1.0 + gate_heads * (1.0 - gate_sig))
    back_gate_in = back_gate_in.astype(BF16).reshape(tokens, vw)
    grad_gate = outer_sum(normed, back_gate_in).astype(BF16)
    grad_out = outer_sum(gated, hidden_bf).astype(BF16)
    early = jnp.concatenate([grad_gate, grad_out.reshape(width, -1)], axis=1)
    if direct:
        given, kept = pair_parts(early)
        early = pair_total(pair_sent(given), kept)[0]
    else:
        early = lax.psum_scatter(early, "fsdp", scatter_dimension=0, tiled=True)
    back_gated, early, grad_up = lax.optimization_barrier((back_gated, early, grad_up))
    early_blocks = chip_blocks(early) if direct else [early]
    up_sent = sent_round(grad_up[None])
    mlp_blocks = seq_blocks(mlp_out)
    back_proj, small = mix_backward(pre, gate, logits, decay, taps, head_gain, saved, back_gated, heads, dk, dv)
    back_proj = back_proj.reshape(tokens, core)
    small = jnp.pad(jnp.sum(small, axis=0), ((0, 0), (0, LANES)))
    grad_core = outer_sum(normed, back_proj).astype(BF16)
    if direct:
        given, kept = pair_parts(grad_core, small.astype(BF16))
        given, back_proj = lax.optimization_barrier((given, back_proj))
        given = pair_sent(given)
    else:
        core_own = lax.psum_scatter(grad_core, "fsdp", scatter_dimension=0, tiled=True)
    back_x = back_product(back_proj, mix[:, :core]) + back_product(back_gate_in, mix[:, core:])
    back_x = back_x.astype(BF16)
    if direct:
        given, back_x = lax.optimization_barrier((given, back_x))
        stream_blocks = seq_blocks(back_x.reshape(by_seq + (width,)))
        core_blocks = chip_blocks(*pair_total(given, kept, small.shape[0]))
        *early_blocks, first = lax.optimization_barrier((*early_blocks, core_blocks[0]))
        core_blocks = [first] + core_blocks[1:]
    else:
        stream_blocks = seq_blocks(back_x.reshape(by_seq + (width,)))
    early = add_up(early_blocks).astype(BF16)
    rows_grad = jnp.concatenate([early[:, vw:].reshape(out_held, width), grad_down], axis=0)
    rows_grad = lax.ppermute(rows_grad, ("seq", "fsdp"), swap_pairs(True))[None]
    result = hidden + add_up(mlp_blocks)
    raw_up = in_order(grad_up[None], up_sent, 0)
    raw_up = jnp.concatenate([columns(raw_up, 0, ff), columns(raw_up, ff, ff)], axis=1).astype(F32)
    grad_post = jnp.sum(raw_up * upmap.astype(F32), axis=1) / postnorm.astype(F32)
    if direct:
        *core_blocks, raw_up, result = lax.optimization_barrier((*core_blocks, raw_up, result))
        total = add_up(core_blocks)
        small_own, core_own = total[held:].astype(BF16), total[:held].astype(BF16)
    else:
        small_own = small_sum(small).astype(BF16)
    mix_own = jnp.concatenate(
        [jnp.concatenate([core_own, early[:, :vw]], axis=1), jnp.pad(small_own, ((0, 0), (0, vw)))], axis=0
    )
    rows_sent = sent_round(rows_grad)
    mix_sent = sent_round(mix_own[None])
    stream_grad = back_hidden + unit_back(stream, add_up(stream_blocks) * pre_gain)
    rows_grad = in_order(rows_grad, rows_sent, 0).astype(F32)
    *mix_sent, stream_grad, rows_grad = lax.optimization_barrier((*mix_sent, stream_grad, rows_grad))
    grad_all = in_order(mix_own[None], mix_sent, 0)
    small = grad_all[:, held:].astype(F32)
    grad_all = grad_all[:, :held]
    raw_mix = jnp.concatenate(
        [columns(grad_all, 0, kw), columns(grad_all, kw, kw), columns(grad_all, 2 * kw, vw), columns(grad_all, core, vw)], axis=1
    ).astype(F32)
    raw_rate = jnp.concatenate(
        [columns(grad_all, wide, heads), columns(grad_all, wide + heads, heads)], axis=1
    ).astype(F32)
    grad_pre = jnp.sum(raw_mix * mixing.astype(F32), axis=1) + jnp.sum(raw_rate * ratemap.astype(F32), axis=1)
    grad_pre = grad_pre / prenorm.astype(F32)
    taps_rows = small[:, : convtaps.shape[0]]
    conv_all = jnp.concatenate(
        [columns(taps_rows, 0, kw), columns(taps_rows, kw, kw), columns(taps_rows, 2 * kw, vw)], axis=1
    )
    owner = lax.axis_index("fsdp")
    grad_conv = cut(conv_all, owner * convtaps.shape[1], convtaps.shape[1], 1)
    grad_head = cut(jnp.sum(small[:, 4, :dv], axis=0), owner * headgain.shape[0], headgain.shape[0], 0)
    return (
        result,
        stream_grad,
        grad_pre,
        raw_mix,
        raw_rate,
        grad_conv,
        small[:, 5, heads : 2 * heads].reshape(-1),
        small[:, 6, heads : 2 * heads].reshape(-1),
        grad_head,
        rows_grad[:, :out_held].reshape(outmap.shape),
        grad_post,
        raw_up,
        rows_grad[:, out_held:].reshape(downmap.shape),
    )


def solution(mesh):
    tokens, rows = P("fsdp", "seq", None), P("fsdp", None)
    return jax.shard_map(
        shards,
        mesh=mesh,
        in_specs=(
            tokens, tokens, P("fsdp"), rows, rows, P(None, "fsdp"), P(), P(), P("fsdp"), rows, P("fsdp"), rows, rows,
        ),
        out_specs=(
            tokens, tokens, P("fsdp"), rows, rows, P(None, "fsdp"), P(), P(), P("fsdp"), rows, P("fsdp"), rows, rows,
        ),
        check_vma=False,
    )
```

```python
import functools

import jax
import jax.numpy as jnp
from jax import lax
from jax.experimental import pallas as pl
from jax.experimental.pallas import tpu as pltpu
from jax.sharding import PartitionSpec as P

CHUNK = 128
LANES = 128
PAD = 8
EPSILON = 1e-06
F32 = jnp.float32
BF16 = jnp.bfloat16
INTERPRET = False
UNROLL = 1
PASSES = {"inv": 3, "kk": 3, "qk": 3, "chain": 3, "out": 3, "back": 3, "grad": 3}


def halves(value):
    high = value.astype(BF16)
    return high, (value - high.astype(F32)).astype(BF16)


def contract(left, right, dims, site):
    def dot(a, b):
        return lax.dot_general(a, b, (dims, ((), ())), preferred_element_type=F32)

    if PASSES[site] == 1:
        return dot(left.astype(BF16), right.astype(BF16))
    left, right = halves(left), halves(right)
    return dot(left[0], right[0]) + (dot(left[0], right[1]) + dot(left[1], right[0]))


def mm(left, right, site):
    return contract(left, right, ((1,), (0,)), site)


def mt(left, right, site):
    return contract(left, right, ((1,), (1,)), site)


def tm(left, right, site):
    return contract(left, right, ((0,), (0,)), site)


def thirds(value):
    high, rest = halves(value)
    low = (value - high.astype(F32) - rest.astype(F32)).astype(BF16)
    return high, rest, low


def exact(flags, value, dims, flags_first=True):
    total = None
    for part in thirds(value)[::-1]:
        pair = (flags, part) if flags_first else (part, flags)
        term = lax.dot_general(*pair, (dims, ((), ())), preferred_element_type=F32)
        total = term if total is None else total + term
    return total


def sigmoid(value):
    return 1.0 / (1.0 + jnp.exp(-value))


def soft_plus(value):
    return jnp.maximum(value, 0.0) + jnp.log1p(jnp.exp(-jnp.abs(value)))


def rates_of(logits, decay_ref, heads):
    lane = lax.broadcasted_iota(jnp.int32, logits.shape, 1)
    decays = decay_ref[0:1] * soft_plus(logits + decay_ref[1:2])
    return jnp.where(lane < heads, sigmoid(logits), decays)


def iotas(size):
    rows = lax.broadcasted_iota(jnp.int32, (size, size), 0)
    cols = lax.broadcasted_iota(jnp.int32, (size, size), 1)
    return rows, cols


def unit_inverse(lower, rows, cols):
    size = lower.shape[0]
    inverse = jnp.where(rows == cols, 1.0, 0.0) - jnp.where(rows // 2 == cols // 2, lower, 0.0)
    width = 2
    while width < size:
        joins = (rows // (2 * width) == cols // (2 * width)) & (rows // width != cols // width)
        inverse = inverse - mm(mm(inverse, jnp.where(joins, lower, 0.0), "inv"), inverse, "inv")
        width *= 2
    return inverse


def conv_window(window, taps, span):
    total = taps[0:1] * window[PAD - 3 : PAD - 3 + span]
    for offset in range(1, 4):
        start = PAD - 3 + offset
        total = total + taps[offset : offset + 1] * window[start : start + span]
    return total


def fades(decay, rows, cols):
    span = rows.shape[0]
    ones_below = jnp.where(rows >= cols, 1.0, 0.0).astype(BF16)
    wide = jnp.broadcast_to(decay, (span, span))
    by_row = exact(ones_below, wide, ((1,), (0,)))
    by_col = exact(ones_below, wide, ((0,), (1,)), False)
    gap = by_row - by_col
    causal = rows >= cols
    fade = jnp.where(causal, jnp.exp(jnp.where(causal, gap, 0.0)), 0.0)
    total = by_row[span - 1 : span, 0:1]
    grown = jnp.exp(by_row[:, 0:1])
    left = jnp.exp(total - by_row[:, 0:1])
    return fade, grown, left, jnp.exp(total)


def turned_rows(here, i, chunk, length, peers):
    per = length // peers // chunk
    slot = lax.rem(here - i // per + peers, peers)
    return pl.ds(pl.multiple_of((slot * per + lax.rem(i, per)) * chunk, chunk), chunk)


def forward_kernel(
    here_ref, pre_ref, gate_ref, logit_ref, decay_ref, taps_ref, gain_ref,
    gated_ref, out_ref, fresh_ref, state_ref, inv_ref, att_ref,
    xp, qs, kb, ke, vb, rate_ref, carried, *, heads, dk, dv, chunk, peers
):
    length = pre_ref.shape[0]
    size = chunk
    blocks = length // size
    qw = heads * dk
    xp[0:PAD] = jnp.zeros((PAD, xp.shape[1]), F32)
    for i in range(blocks):
        there = turned_rows(here_ref[0], jnp.int32(i), size, length, peers)
        xp[PAD + i * size : PAD + (i + 1) * size] = pre_ref[there, :].astype(F32)
        rate_ref[i * size : (i + 1) * size] = rates_of(logit_ref[there, :], decay_ref, heads)
    carried[...] = jnp.zeros_like(carried)
    rows, cols = iotas(size)

    def prepare(i, carry):
        r0 = pl.multiple_of(i * size, size)
        rates = rate_ref[pl.ds(r0, size), :]
        for h in range(heads):
            def act(start, width):
                c = conv_window(xp[pl.ds(r0, size + PAD), start : start + width], taps_ref[:, start : start + width], size)
                return c * sigmoid(c)

            q = act(h * dk, dk)
            k = act(qw + h * dk, dk)
            v = act(2 * qw + h * dv, dv)
            q = q * (lax.rsqrt(jnp.sum(q * q, axis=1, keepdims=True) + EPSILON) * dk ** (-0.5))
            k = k * lax.rsqrt(jnp.sum(k * k, axis=1, keepdims=True) + EPSILON)
            beta = rates[:, h : h + 1]
            fade, grown, left, _ = fades(rates[:, heads + h : heads + h + 1], rows, cols)
            lower = jnp.where(rows > cols, beta * fade * mt(k, k, "kk"), 0.0)
            inv_ref[i, h] = unit_inverse(lower, rows, cols)
            att_ref[i, h] = fade * mt(q, k, "qk")
            span = pl.ds(r0, size)
            qs[span, h * dk : (h + 1) * dk] = grown * q
            kb[span, h * dk : (h + 1) * dk] = (beta * grown) * k
            ke[span, h * dk : (h + 1) * dk] = left * k
            vb[span, h * dv : (h + 1) * dv] = beta * v
        return carry

    lax.fori_loop(0, blocks, prepare, 0, unroll=UNROLL)

    def advance(i, carry):
        r0 = pl.multiple_of(i * size, size)
        there = turned_rows(here_ref[0], i, size, length, peers)
        span = pl.ds(r0, size)
        rates = rate_ref[span, :]
        for h in range(heads):
            state = carried[h]
            state_ref[i, h] = state
            ks = slice(h * dk, (h + 1) * dk)
            vs = slice(h * dv, (h + 1) * dv)
            fresh = mm(inv_ref[i, h], vb[span, vs] - mm(kb[span, ks], state, "chain"), "chain")
            fresh_ref[span, vs] = fresh
            out = mm(qs[span, ks], state, "out") + mm(att_ref[i, h], fresh, "out")
            out_ref[there, vs] = out
            end = jnp.exp(jnp.sum(rates[:, heads + h : heads + h + 1], axis=0, keepdims=True))
            carried[h] = end * state + tm(ke[span, ks], fresh, "chain")
            scale = lax.rsqrt(jnp.mean(out * out, axis=1, keepdims=True) + EPSILON)
            gate = gate_ref[there, vs]
            gated_ref[there, vs] = (out * scale * gain_ref[...] * gate * sigmoid(gate)).astype(BF16)
        return carry

    lax.fori_loop(0, blocks, advance, 0, unroll=UNROLL)


def backward_kernel(
    here_ref, pre_ref, gate_ref, logit_ref, decay_ref, taps_ref, gain_ref, out_ref, fresh_ref, state_ref, inv_ref, att_ref, dgated_ref,
    dproj_ref, small_ref,
    xp, qn, kn, vn, dout, dright, dstate, dconv, rate_ref, drate_ref, carried, *, heads, dk, dv, chunk, peers
):
    length = pre_ref.shape[0]
    size = chunk
    blocks = length // size
    qw = heads * dk
    wide = xp.shape[1]
    xp[0:PAD] = jnp.zeros((PAD, wide), F32)
    for i in range(blocks):
        there = turned_rows(here_ref[0], jnp.int32(i), size, length, peers)
        xp[PAD + i * size : PAD + (i + 1) * size] = pre_ref[there, :].astype(F32)
        rate_ref[i * size : (i + 1) * size] = rates_of(logit_ref[there, :], decay_ref, heads)
    dconv[length:] = jnp.zeros((PAD, wide), F32)
    carried[...] = jnp.zeros_like(carried)
    small_ref[...] = jnp.zeros_like(small_ref)
    drate_ref[...] = jnp.zeros_like(drate_ref)
    rows, cols = iotas(size)

    def conv_of(r0, start, width):
        return conv_window(xp[pl.ds(r0, size + PAD), start : start + width], taps_ref[:, start : start + width], size)

    def prepare(i, carry):
        r0 = pl.multiple_of(i * size, size)
        span = pl.ds(r0, size)
        there = turned_rows(here_ref[0], i, size, length, peers)
        for h in range(heads):
            vs = slice(h * dv, (h + 1) * dv)
            ks = slice(h * dk, (h + 1) * dk)
            c = conv_of(r0, h * dk, dk)
            q = c * sigmoid(c)
            qn[span, ks] = q * (lax.rsqrt(jnp.sum(q * q, axis=1, keepdims=True) + EPSILON) * dk ** (-0.5))
            c = conv_of(r0, qw + h * dk, dk)
            k = c * sigmoid(c)
            kn[span, ks] = k * lax.rsqrt(jnp.sum(k * k, axis=1, keepdims=True) + EPSILON)
            c = conv_of(r0, 2 * qw + h * dv, dv)
            vn[span, vs] = c * sigmoid(c)
            out = out_ref[there, vs]
            scale = lax.rsqrt(jnp.mean(out * out, axis=1, keepdims=True) + EPSILON)
            unit = out * scale
            gate = gate_ref[there, vs]
            sig = sigmoid(gate)
            dy = dgated_ref[there, vs]
            dproj_ref[there, wide + LANES + h * dv : wide + LANES + (h + 1) * dv] = (
                dy * unit * gain_ref[...] * sig * (1.0 + gate * (1.0 - sig))
            ).astype(BF16)
            dz = dy * gate * sig
            small_ref[4:5, 0:dv] += jnp.sum(dz * unit, axis=0, keepdims=True)
            dn = dz * gain_ref[...]
            dout[span, vs] = scale * (dn - unit * jnp.mean(unit * dn, axis=1, keepdims=True))
        return carry

    lax.fori_loop(0, blocks, prepare, 0, unroll=UNROLL)

    def retreat(step, carry):
        i = blocks - 1 - step
        r0 = pl.multiple_of(i * size, size)
        span = pl.ds(r0, size)
        rates = rate_ref[span, :]
        for h in range(heads):
            vs = slice(h * dv, (h + 1) * dv)
            ks = slice(h * dk, (h + 1) * dk)
            q, k = qn[span, ks], kn[span, ks]
            beta = rates[:, h : h + 1]
            fade, grown, left, end = fades(rates[:, heads + h : heads + h + 1], rows, cols)
            attend = att_ref[i, h]
            after = carried[h]
            dstate[i, h] = after
            do = dout[span, vs]
            dfresh = tm(attend, do, "back") + mm(left * k, after, "back")
            dr = tm(inv_ref[i, h], dfresh, "back")
            dright[span, vs] = dr
            carried[h] = tm(grown * q, do, "back") + end * after - tm((beta * grown) * k, dr, "back")
        return carry

    lax.fori_loop(0, blocks, retreat, 0, unroll=UNROLL)

    def collect(i, carry):
        r0 = pl.multiple_of(i * size, size)
        span = pl.ds(r0, size)
        rates = rate_ref[span, :]
        ones = jnp.ones((size, size), BF16)
        ones_below = jnp.where(rows >= cols, 1.0, 0.0).astype(BF16)
        for h in range(heads):
            vs = slice(h * dv, (h + 1) * dv)
            ks = slice(h * dk, (h + 1) * dk)
            q, k, v = qn[span, ks], kn[span, ks], vn[span, vs]
            beta = rates[:, h : h + 1]
            fade, grown, left, end = fades(rates[:, heads + h : heads + h + 1], rows, cols)
            below = jnp.where(rows > cols, fade, 0.0)
            state, after = state_ref[i, h], dstate[i, h]
            do, dr, fresh = dout[span, vs], dright[span, vs], fresh_ref[span, vs]
            d_att = mt(do, fresh, "grad")
            d_low = -mt(dr, fresh, "grad")
            pairs = below * mt(k, k, "kk")
            scores = att_ref[i, h]
            d_qk = fade * d_att
            d_kk = beta * below * d_low
            d_qs = mt(do, state, "grad")
            d_ke = mt(fresh, after, "grad")
            d_kb = -mt(dr, state, "grad")
            gaps = d_low * (beta * pairs) + d_att * scores
            dbeta = jnp.sum(d_low * pairs, axis=1, keepdims=True)
            dbeta = dbeta + grown * jnp.sum(d_kb * k, axis=1, keepdims=True)
            dbeta = dbeta + jnp.sum(dr * v, axis=1, keepdims=True)
            dq = mm(d_qk, k, "grad") + grown * d_qs
            dk_ = mm(d_kk, k, "grad") + tm(d_kk, k, "grad") + tm(d_qk, q, "grad") + (beta * grown) * d_kb + left * d_ke
            dv_ = beta * dr
            from_end = left * jnp.sum(d_ke * k, axis=1, keepdims=True)
            dcum = jnp.sum(gaps, axis=1, keepdims=True) - exact(ones, gaps, ((0,), (0,)), False)[:, 0:1]
            dcum = dcum + grown * jnp.sum(d_qs * q, axis=1, keepdims=True)
            dcum = dcum + (beta * grown) * jnp.sum(d_kb * k, axis=1, keepdims=True) - from_end
            d_end = jnp.sum(from_end, axis=0, keepdims=True) + end * jnp.sum(
                jnp.sum(state * after, axis=1, keepdims=True), axis=0, keepdims=True
            )
            ddecay = exact(ones_below, jnp.broadcast_to(dcum, (size, size)), ((0,), (0,)))[:, 0:1] + d_end
            drate_ref[span, h : h + 1] = dbeta
            drate_ref[span, heads + h : heads + h + 1] = ddecay

            def back(start, width, grad, factor):
                c = conv_of(r0, start, width)
                sig = sigmoid(c)
                if factor is not None:
                    act = c * sig
                    scale = lax.rsqrt(jnp.sum(act * act, axis=1, keepdims=True) + EPSILON)
                    unit = act * scale
                    grad = grad * factor
                    grad = scale * (grad - unit * jnp.sum(unit * grad, axis=1, keepdims=True))
                dconv[span, start : start + width] = grad * sig * (1.0 + c * (1.0 - sig))

            back(h * dk, dk, dq, dk ** (-0.5))
            back(qw + h * dk, dk, dk_, 1.0)
            back(2 * qw + h * dv, dv, dv_, None)
        return carry

    lax.fori_loop(0, blocks, collect, 0, unroll=UNROLL)

    def unconv(i, carry):
        r0 = pl.multiple_of(i * size, size)
        span = pl.ds(r0, size)
        there = turned_rows(here_ref[0], i, size, length, peers)
        grads, rates, logits = drate_ref[span, :], rate_ref[span, :], logit_ref[there, :]
        lane = lax.broadcasted_iota(jnp.int32, grads.shape, 1)
        slope = jnp.where(lane < heads, rates * (1.0 - rates), decay_ref[0:1] * sigmoid(logits + decay_ref[1:2]))
        back_rates = grads * slope
        dproj_ref[there, wide : wide + LANES] = back_rates.astype(BF16)
        small_ref[5:6, 0:LANES] += jnp.sum(grads * rates, axis=0, keepdims=True)
        small_ref[6:7, 0:LANES] += jnp.sum(back_rates, axis=0, keepdims=True)
        step = min(256, wide)
        for start in range(0, wide, step):
            cs = slice(start, start + step)
            dwin = dconv[pl.ds(r0, size + PAD), cs]
            xwin = xp[pl.ds(r0, size + PAD), cs]
            taps = taps_ref[:, cs]
            total = None
            for j in range(4):
                term = taps[j : j + 1] * dwin[3 - j : 3 - j + size]
                total = term if total is None else total + term
                small_ref[j : j + 1, cs] += jnp.sum(
                    dwin[0:size] * xwin[PAD - 3 + j : PAD - 3 + j + size], axis=0, keepdims=True
                )
            dproj_ref[there, cs] = total.astype(BF16)
        return carry

    lax.fori_loop(0, blocks, unconv, 0, unroll=UNROLL)


def here_scalar():
    return lax.axis_index("seq").astype(jnp.int32).reshape(1)


def chunk_of(length):
    chunk = CHUNK
    while length % chunk:
        chunk //= 2
    return chunk


def whole(*dims):
    return pl.BlockSpec((None,) + dims, lambda b, here: (b,) + (0,) * len(dims))


def fixed(*dims):
    return pl.BlockSpec(dims, lambda b, here: (0,) * len(dims))


def mix_forward(pre, gate, logits, decay, taps, gain, heads, dk, dv):
    count, length, wide = pre.shape
    peers = lax.axis_size("seq")
    chunk = chunk_of(length // peers)
    blocks = length // chunk
    vw = heads * dv
    square = (blocks, heads, chunk, chunk)
    return pl.pallas_call(
        functools.partial(forward_kernel, heads=heads, dk=dk, dv=dv, chunk=chunk, peers=peers),
        grid_spec=pltpu.PrefetchScalarGridSpec(num_scalar_prefetch=1, grid=(count,), in_specs=[
            whole(length, wide), whole(length, vw), whole(length, LANES),
            fixed(*decay.shape), fixed(*taps.shape), fixed(*gain.shape),
        ],
        out_specs=[
            whole(length, vw), whole(length, vw), whole(length, vw), whole(blocks, heads, dk, dv), whole(*square), whole(*square),
        ],
        scratch_shapes=[
            pltpu.VMEM((length + PAD, wide), F32),
            pltpu.VMEM((length, heads * dk), F32),
            pltpu.VMEM((length, heads * dk), F32),
            pltpu.VMEM((length, heads * dk), F32),
            pltpu.VMEM((length, vw), F32),
            pltpu.VMEM((length, LANES), F32),
            pltpu.VMEM((heads, dk, dv), F32),
        ]),
        out_shape=[
            jax.ShapeDtypeStruct((count, length, vw), BF16),
            jax.ShapeDtypeStruct((count, length, vw), F32),
            jax.ShapeDtypeStruct((count, length, vw), F32),
            jax.ShapeDtypeStruct((count, blocks, heads, dk, dv), F32),
            jax.ShapeDtypeStruct((count,) + square, F32),
            jax.ShapeDtypeStruct((count,) + square, F32),
        ],
        cost_estimate=pl.CostEstimate(flops=10**10, bytes_accessed=32 * 2**20, transcendentals=10**6),
        interpret=INTERPRET,
    )(here_scalar(), pre, gate, logits, decay, taps, gain)


def mix_backward(pre, gate, logits, decay, taps, gain, saved, dgated, heads, dk, dv):
    count, length, wide = pre.shape
    peers = lax.axis_size("seq")
    chunk = chunk_of(length // peers)
    blocks = length // chunk
    vw = heads * dv
    square = (blocks, heads, chunk, chunk)
    return pl.pallas_call(
        functools.partial(backward_kernel, heads=heads, dk=dk, dv=dv, chunk=chunk, peers=peers),
        grid_spec=pltpu.PrefetchScalarGridSpec(num_scalar_prefetch=1, grid=(count,), in_specs=[
            whole(length, wide), whole(length, vw), whole(length, LANES),
            fixed(*decay.shape), fixed(*taps.shape), fixed(*gain.shape),
            whole(length, vw), whole(length, vw), whole(blocks, heads, dk, dv), whole(*square), whole(*square), whole(length, vw),
        ],
        out_specs=[whole(length, wide + LANES + vw), whole(8, wide)],
        scratch_shapes=[
            pltpu.VMEM((length + PAD, wide), F32),
            pltpu.VMEM((length, heads * dk), F32),
            pltpu.VMEM((length, heads * dk), F32),
            pltpu.VMEM((length, vw), F32),
            pltpu.VMEM((length, vw), F32),
            pltpu.VMEM((length, vw), F32),
            pltpu.VMEM((blocks, heads, dk, dv), F32),
            pltpu.VMEM((length + PAD, wide), F32),
            pltpu.VMEM((length, LANES), F32),
            pltpu.VMEM((length, LANES), F32),
            pltpu.VMEM((heads, dk, dv), F32),
        ]),
        out_shape=[
            jax.ShapeDtypeStruct((count, length, wide + LANES + vw), BF16),
            jax.ShapeDtypeStruct((count, 8, wide), F32),
        ],
        cost_estimate=pl.CostEstimate(flops=10**10, bytes_accessed=32 * 2**20, transcendentals=2 * 10**6),
        interpret=INTERPRET,
    )(here_scalar(), pre, gate, logits, decay, taps, gain, *saved, dgated)


def unit_rows(values):
    return values * lax.rsqrt(jnp.mean(values * values, axis=-1, keepdims=True) + EPSILON)


def unit_back(values, grad):
    scale = lax.rsqrt(jnp.mean(values * values, axis=-1, keepdims=True) + EPSILON)
    unit = values * scale
    return scale * (grad - unit * jnp.mean(unit * grad, axis=-1, keepdims=True))


def product(left, right):
    return jnp.dot(left, right, preferred_element_type=F32)


def outer_sum(left, right):
    return lax.dot_general(left, right, (((0,), (0,)), ((), ())), preferred_element_type=F32)


def back_product(left, right):
    return lax.dot_general(left, right, (((1,), (1,)), ((), ())), preferred_element_type=F32)


def cut(array, start, size, axis):
    return lax.dynamic_slice_in_dim(array, start, size, axis)


def after(value, *others):
    return lax.optimization_barrier((value,) + others)[0]


def turned(value, by):
    peers = lax.axis_size("seq")
    return lax.ppermute(value, "seq", [(i, (i + by) % peers) for i in range(peers)])


def sent_round(piece):
    return [turned(piece, by) for by in range(1, lax.axis_size("seq"))]


def seq_join(piece, others):
    return jnp.concatenate([piece] + others, axis=1)


def seq_blocks(partial):
    peers = lax.axis_size("seq")
    length = partial.shape[1] // peers
    blocks = [partial[:, turn * length : (turn + 1) * length] for turn in range(peers)]
    return blocks[:1] + [turned(blocks[peers - by], by) for by in range(1, peers)]


def add_up(blocks):
    total = blocks[0].astype(F32)
    for block in blocks[1:]:
        total = total + block.astype(F32)
    return total


def swap_pairs(invert):
    peers, owners = lax.axis_size("seq"), lax.axis_size("fsdp")
    group = owners // peers
    pairs = []
    for s in range(peers):
        for f in range(owners):
            holder = (f % peers) * owners + s * group + f // peers
            pairs.append((s * owners + f, holder) if invert else (holder, s * owners + f))
    return pairs


def owners_piece(shard):
    rows = shard.shape[0] // lax.axis_size("seq")
    return cut(shard, lax.axis_index("seq") * rows, rows, 0)


def small_sum(value):
    owners = lax.axis_size("fsdp")
    step = 1
    while step < owners:
        value = value + lax.ppermute(value, "fsdp", [(i, i ^ step) for i in range(owners)])
        step *= 2
    return value


def pair_parts(grad, rider=None):
    owners = lax.axis_size("fsdp")
    parity = lax.axis_index("fsdp") % 2
    wide = grad.shape[1]
    grad = grad.reshape(owners // 2, 2, -1, wide)
    given = cut(grad, 1 - parity, 1, 1).reshape(-1, wide)
    kept = cut(grad, parity, 1, 1).reshape(-1, wide)
    if rider is None:
        return given, kept
    return jnp.concatenate([given, rider]), jnp.concatenate([kept, rider])


def pair_sent(given):
    return lax.ppermute(given, "fsdp", [(i, i ^ 1) for i in range(lax.axis_size("fsdp"))])


def pair_total(given, kept, riding=0):
    total = (kept.astype(F32) + given.astype(F32)).astype(BF16)
    size = total.shape[0] - riding
    blocks = total[:size].reshape(lax.axis_size("fsdp") // 2, -1, total.shape[1])
    return (blocks, total[size:]) if riding else (blocks,)


def chip_blocks(both, rider=None):
    owners = lax.axis_size("fsdp")
    groups = owners // 2
    place = lax.axis_index("fsdp") // 2

    def block(at):
        part = cut(both, at, 1, 0)[0]
        return part if rider is None else jnp.concatenate([part, rider])

    blocks = [block(place)]
    for by in range(1, groups):
        pairs = [(i, (i + 2 * by) % owners) for i in range(owners)]
        blocks.append(lax.ppermute(block((place + by) % groups), "fsdp", pairs))
    return blocks


def spread_kernel(here_ref, *refs, moves, rows, peers):
    pieces, (weight_ref, full_ref, sums_ref) = refs[:peers], refs[peers:]
    sums_ref[...] = jnp.zeros_like(sums_ref)
    for turn, piece_ref in enumerate(pieces):
        place = lax.rem(here_ref[0] - turn + peers, peers)
        for source, width, target in moves:
            at = pl.ds(pl.multiple_of(target + place * width, LANES), width)
            part = piece_ref[0:rows, source : source + width].astype(F32)
            full_ref[:, at] = part
            total = jnp.sum(part * weight_ref[:, at].astype(F32), axis=1, keepdims=True)
            sums_ref[...] += jnp.broadcast_to(total, sums_ref.shape)


def spread_columns(pieces, weight, moves):
    rows = weight.shape[0]
    return pl.pallas_call(
        functools.partial(spread_kernel, moves=moves, rows=rows, peers=len(pieces)),
        grid_spec=pltpu.PrefetchScalarGridSpec(
            num_scalar_prefetch=1,
            grid=(1,),
            in_specs=[fixed(*piece.shape) for piece in pieces] + [fixed(*weight.shape)],
            out_specs=[fixed(*weight.shape), fixed(rows, LANES)],
        ),
        out_shape=[jax.ShapeDtypeStruct(weight.shape, F32), jax.ShapeDtypeStruct((rows, LANES), F32)],
        cost_estimate=pl.CostEstimate(flops=10**6, bytes_accessed=8 * weight.size, transcendentals=0),
        interpret=INTERPRET,
    )(here_scalar(), *pieces, weight)


def stack_kernel(here_ref, *refs, cuts, peers):
    pieces, outs = refs[:peers], refs[peers:]
    for turn, piece_ref in enumerate(pieces):
        place = lax.rem(here_ref[0] - turn + peers, peers)
        start = 0
        for size, out_ref in zip(cuts, outs):
            out_ref[place] = piece_ref[start : start + size].astype(F32)
            start += size


def stack_rows(pieces, cuts):
    peers, wide = len(pieces), pieces[0].shape[1]
    return pl.pallas_call(
        functools.partial(stack_kernel, cuts=cuts, peers=peers),
        grid_spec=pltpu.PrefetchScalarGridSpec(
            num_scalar_prefetch=1,
            grid=(1,),
            in_specs=[fixed(*piece.shape) for piece in pieces],
            out_specs=[fixed(peers, size, wide) for size in cuts],
        ),
        out_shape=[jax.ShapeDtypeStruct((peers, size, wide), F32) for size in cuts],
        cost_estimate=pl.CostEstimate(flops=10**6, bytes_accessed=24 * pieces[0].size, transcendentals=0),
        interpret=INTERPRET,
    )(here_scalar(), *pieces)


def ordered(pieces):
    peers = len(pieces)
    return jnp.stack(pieces)[(lax.axis_index("seq") - jnp.arange(peers)) % peers]


def columns(stacked, start, width):
    part = stacked[:, :, start : start + width]
    return jnp.transpose(part, (1, 0, 2)).reshape(part.shape[1], -1)


def shards(
    stream, cotangent, prenorm, mixing, ratemap, convtaps, decaylog, decaybias, headgain, outmap, postnorm, upmap, downmap,
):
    count, length, width = stream.shape
    peers, owners = lax.axis_size("seq"), lax.axis_size("fsdp")
    here = lax.axis_index("seq")
    direct = owners <= 8
    all_heads = decaylog.shape[0]
    heads = all_heads // peers
    dv = headgain.shape[0] * owners
    qkv = convtaps.shape[1] * owners
    dk = (qkv // all_heads - dv) // 2
    kw, vw = heads * dk, heads * dv
    wide = 2 * kw + vw
    core = wide + LANES
    ff = downmap.shape[0] * owners // peers
    tokens = count * length * peers
    by_seq = (count, peers * length)
    held = mixing.shape[0]
    out_held = outmap.shape[0] // peers

    taps_part = convtaps.reshape(held, -1)
    gain_part = jnp.pad(headgain, (0, held - headgain.shape[0]))[:, None]
    used = 2 * heads + taps_part.shape[1] + 1
    mix_part = jnp.concatenate(
        [
            cut(mixing, here * kw, kw, 1),
            cut(mixing, all_heads * dk + here * kw, kw, 1),
            cut(mixing, 2 * all_heads * dk + here * vw, vw, 1),
            cut(ratemap, here * heads, heads, 1),
            cut(ratemap, all_heads + here * heads, heads, 1),
            taps_part,
            gain_part,
            jnp.zeros((held, LANES - used), BF16),
            cut(mixing, qkv + here * vw, vw, 1),
        ],
        axis=1,
    )
    mix = lax.all_gather(mix_part, "fsdp", axis=0, tiled=True)
    gains = after(jnp.stack([prenorm, postnorm]), mix_part)
    gains = lax.all_gather(gains, "fsdp", axis=1, tiled=True).astype(F32)
    pre_gain, post_gain = gains[0], gains[1]

    normed_own = (unit_rows(stream) * pre_gain).astype(BF16)
    normed = seq_join(normed_own, sent_round(normed_own))
    cot_own = cotangent.astype(BF16)
    cot_own, normed = lax.optimization_barrier((cot_own, normed))
    cot_sent = sent_round(cot_own)
    rows_piece = jnp.concatenate([owners_piece(outmap), owners_piece(downmap)], axis=0)
    rows_piece = lax.ppermute(rows_piece, ("seq", "fsdp"), swap_pairs(False))
    up_part = jnp.concatenate([cut(upmap, here * ff, ff, 1), cut(upmap, (peers + here) * ff, ff, 1)], axis=1)
    rows_piece, up_part, normed, mix, *cot_sent = lax.optimization_barrier((rows_piece, up_part, normed, mix, *cot_sent))
    rows_all = lax.all_gather(rows_piece, "fsdp", axis=0, tiled=False)
    up = lax.all_gather(up_part, "fsdp", axis=0, tiled=True)
    normed = normed.reshape(tokens, width)

    extra = mix[:, wide:core]
    taps_all = extra[:, 2 * heads : 2 * heads + taps_part.shape[1]].reshape(owners, convtaps.shape[0], -1)
    taps_all = jnp.transpose(taps_all, (1, 0, 2)).reshape(convtaps.shape[0], -1)
    taps = jnp.concatenate(
        [
            cut(taps_all, here * kw, kw, 1),
            cut(taps_all, all_heads * dk + here * kw, kw, 1),
            cut(taps_all, 2 * all_heads * dk + here * vw, vw, 1),
        ],
        axis=1,
    ).astype(F32)
    head_gain = extra[:, used - 1].reshape(owners, held)[:, : headgain.shape[0]].reshape(1, dv).astype(F32)
    decay = jnp.stack([-jnp.exp(cut(decaylog, here * heads, heads, 0)), cut(decaybias, here * heads, heads, 0)])
    decay = jnp.pad(decay, ((0, 6), (heads, LANES - 2 * heads)))

    pre = product(normed, mix[:, :wide]).astype(BF16).reshape(by_seq + (wide,))
    gate = product(normed, mix[:, core:]).reshape(by_seq + (vw,))
    logits = product(normed, extra).reshape(by_seq + (LANES,))
    gated, *saved = mix_forward(pre, gate, logits, decay, taps, head_gain, heads, dk, dv)
    gated = gated.reshape(tokens, vw)
    out_rows = rows_all[:, :out_held].reshape(vw, width)
    down = rows_all[:, out_held:].reshape(ff, width)
    hidden = stream + add_up(seq_blocks(product(gated, out_rows).astype(BF16).reshape(by_seq + (width,))))

    post_own = (unit_rows(hidden) * post_gain).astype(BF16)
    post_sent = sent_round(post_own)
    cot_bf = seq_join(cot_own, cot_sent).reshape(tokens, width)
    back_act = back_product(cot_bf, down)
    *post_sent, back_act = lax.optimization_barrier((*post_sent, back_act))
    post = seq_join(post_own, post_sent).reshape(tokens, width)
    gate_part = product(post, up[:, :ff])
    up_half = product(post, up[:, ff:])
    sig = jax.nn.sigmoid(gate_part)
    mlp_act = (gate_part * sig * up_half).astype(BF16)
    back_gate = (back_act * up_half * sig * (1.0 + gate_part * (1.0 - sig))).astype(BF16)
    back_up = (back_act * gate_part * sig).astype(BF16)
    back_both = jnp.concatenate([back_gate, back_up], axis=1)
    back_part, back_both = lax.optimization_barrier((back_product(back_both, up).astype(BF16), back_both))
    back_blocks = seq_blocks(back_part.reshape(by_seq + (width,)))
    grad_up = outer_sum(post, back_both).astype(BF16)
    *back_blocks, token = lax.optimization_barrier((*back_blocks, grad_up))
    grad_up = lax.psum_scatter(grad_up, "fsdp", scatter_dimension=0, tiled=True)
    back_hidden = cotangent + unit_back(hidden, add_up(back_blocks) * post_gain)
    hidden_own = back_hidden.astype(BF16)
    hidden_sent = sent_round(hidden_own)
    mlp_act_late = after(mlp_act, token)
    grad_down = outer_sum(mlp_act_late, cot_bf).astype(BF16)
    mlp_out = product(mlp_act_late, down).astype(BF16).reshape(by_seq + (width,))
    *hidden_sent, mlp_out, grad_down = lax.optimization_barrier((*hidden_sent, mlp_out, grad_down))
    hidden_bf = seq_join(hidden_own, hidden_sent).reshape(tokens, width)
    grad_out = outer_sum(gated, hidden_bf).astype(BF16)
    grad_down, grad_out, grad_up = lax.optimization_barrier((grad_down, grad_out, grad_up))
    grad_down = lax.psum_scatter(grad_down, "fsdp", scatter_dimension=0, tiled=True)
    grad_out = lax.psum_scatter(grad_out, "fsdp", scatter_dimension=0, tiled=True)

    back_gated = back_product(hidden_bf, out_rows).reshape(by_seq + (vw,))
    up_sent = sent_round(grad_up)
    mlp_blocks = seq_blocks(mlp_out)
    back_proj, small = mix_backward(pre, gate, logits, decay, taps, head_gain, saved, back_gated, heads, dk, dv)
    back_proj = back_proj.reshape(tokens, core + vw)
    small = jnp.pad(jnp.sum(small, axis=0), ((0, 0), (0, LANES + vw)))
    grad_mix = outer_sum(normed, back_proj).astype(BF16)
    if direct:
        given, kept = pair_parts(grad_mix, small.astype(BF16))
        given, back_proj = lax.optimization_barrier((given, back_proj))
        given = pair_sent(given)
    else:
        mix_own = lax.psum_scatter(grad_mix, "fsdp", scatter_dimension=0, tiled=True)
        mix_own = jnp.concatenate([mix_own, small_sum(small).astype(BF16)], axis=0)
    back_x = back_product(back_proj, mix).astype(BF16)
    if direct:
        given, back_x = lax.optimization_barrier((given, back_x))
    stream_blocks = seq_blocks(back_x.reshape(by_seq + (width,)))
    if direct:
        mix_blocks = chip_blocks(*pair_total(given, kept, small.shape[0]))
        mix_blocks[0], *others = lax.optimization_barrier((mix_blocks[0], *up_sent, *mlp_blocks))
        up_sent, mlp_blocks = others[: peers - 1], others[peers - 1 :]
    result = hidden + add_up(mlp_blocks)
    raw_up = jnp.stack([grad_up] + up_sent)[(here - jnp.arange(peers)) % peers]
    raw_up = jnp.concatenate([columns(raw_up, 0, ff), columns(raw_up, ff, ff)], axis=1).astype(F32)
    grad_post = jnp.sum(raw_up * upmap.astype(F32), axis=1) / postnorm.astype(F32)
    raw_up, grad_out, grad_down = lax.optimization_barrier((raw_up, grad_out, grad_down))
    rows_grad = jnp.concatenate([grad_out, grad_down], axis=0)
    rows_grad = lax.ppermute(rows_grad, ("seq", "fsdp"), swap_pairs(True))
    if direct:
        *mix_blocks, raw_up, result, rows_grad = lax.optimization_barrier((*mix_blocks, raw_up, result, rows_grad))
        mix_own = add_up(mix_blocks).astype(BF16)
    rows_sent = sent_round(rows_grad)
    mix_sent = sent_round(mix_own)
    stream_grad = back_hidden + unit_back(stream, add_up(stream_blocks) * pre_gain)
    rows_out, rows_down = stack_rows([rows_grad] + rows_sent, (out_held, downmap.shape[0] // peers))
    *mix_sent, stream_grad, rows_out = lax.optimization_barrier((*mix_sent, stream_grad, rows_out))
    mix_all = [mix_own] + mix_sent
    raw_mix, mix_sums = spread_columns(
        mix_all, mixing, ((0, kw, 0), (kw, kw, all_heads * dk), (2 * kw, vw, 2 * all_heads * dk), (core, vw, qkv))
    )
    raw_rate = ordered([piece[:held, wide : wide + 2 * heads] for piece in mix_all]).astype(F32)
    raw_rate = jnp.concatenate([columns(raw_rate, 0, heads), columns(raw_rate, heads, heads)], axis=1)
    grad_pre = (mix_sums[:, 0] + jnp.sum(raw_rate * ratemap.astype(F32), axis=1)) / prenorm.astype(F32)
    small = ordered([piece[held:, :wide] for piece in mix_all]).astype(F32)
    taps_rows = small[:, : convtaps.shape[0]]
    conv_all = jnp.concatenate(
        [columns(taps_rows, 0, kw), columns(taps_rows, kw, kw), columns(taps_rows, 2 * kw, vw)], axis=1
    )
    owner = lax.axis_index("fsdp")
    grad_conv = cut(conv_all, owner * convtaps.shape[1], convtaps.shape[1], 1)
    grad_head = cut(jnp.sum(small[:, 4, :dv], axis=0), owner * headgain.shape[0], headgain.shape[0], 0)
    return (
        result,
        stream_grad,
        grad_pre,
        raw_mix,
        raw_rate,
        grad_conv,
        small[:, 5, heads : 2 * heads].reshape(-1),
        small[:, 6, heads : 2 * heads].reshape(-1),
        grad_head,
        rows_out.reshape(outmap.shape),
        grad_post,
        raw_up,
        rows_down.reshape(downmap.shape),
    )


def solution(mesh):
    tokens, rows = P("fsdp", "seq", None), P("fsdp", None)
    return jax.shard_map(
        shards,
        mesh=mesh,
        in_specs=(
            tokens, tokens, P("fsdp"), rows, rows, P(None, "fsdp"), P(), P(), P("fsdp"), rows, P("fsdp"), rows, rows,
        ),
        out_specs=(
            tokens, tokens, P("fsdp"), rows, rows, P(None, "fsdp"), P(), P(), P("fsdp"), rows, P("fsdp"), rows, rows,
        ),
        check_vma=False,
    )
```
